32 devices in a mesh: kx: 2 (over x), ky: 8 (over z, y), af: 2 (over core).
Axes of the slice: x: 2, y: 2, z: 4, core: 2. Of those that a mesh axis runs over, the one named last changes fastest.
Arguments:
- vertex: float32 [2, 2, 8, 768, 768], P(None, 'kx', 'ky', 'af'), may hold values from -1.2 to 1.2
- bare_vertex: float32 [2, 2, 8, 768, 768], P(None, 'kx', 'ky', 'af'), may hold values from -1.2 to 1.2
- bubble_direct: float32 [2, 2, 8, 768], P(None, 'kx', 'ky'), may hold values from 0.1 to 1
- bubble_crossed: float32 [2, 2, 8, 768], P(None, 'kx', 'ky'), may hold values from 0.1 to 1
- shear_in: int32 [2, 768], replicated, may hold values from 0 to 7, as said below
- shear_out: int32 [2, 768], replicated, may hold values from 0 to 7, as said below
Outputs:
- updated: float32 [2, 2, 8, 768, 768], P(None, 'kx', 'ky', 'af')
The draws below stay inside these ranges and needn't reach their ends.
Inputs may be any that keep to these rules, and one draw needn't show every extreme that they name: `shear_in`: row 0 holds each matrix row's shift of the first momentum component (below 4), row 1 that of the second (below 8). Within each half of the 768 rows, every pair (first shift mod 2, second shift) occurs for exactly 24 rows. `shear_out`: same structure as shear_in.
All inputs are finite; a program needn't handle non-finite values.
Results may differ from the reference program's by a relative error of at most 0.000082.
Values sent between devices are 32-bit elements; how exact they have to be, the bound alone decides.
No kernel may reach another device: no remote copies, remote signals or barrier semaphores. Data moves between devices by JAX's collectives and lax.ppermute only.
A program may use at most 64 MiB of HBM per device.

```python
import math
import jax
import jax.numpy as jnp
from jax import lax

M = 768
HX = 2
GX = 2
QX = 4
QY = 8


def shear_draw(key, salt):
    base_key = jax.random.fold_in(key, salt)
    lower_key, upper_key, high_key = jax.random.split(base_key, 3)
    half_rows = M // 2
    classes = GX * QY
    combos = jnp.concatenate([jax.random.permutation(lower_key, half_rows), jax.random.permutation(upper_key, half_rows)]) % classes
    high_part = jax.random.randint(high_key, (M,), 0, HX)
    shift_x = combos % GX + GX * high_part
    shift_y = combos // GX
    return jnp.stack([shift_x, shift_y]).astype(jnp.int32)


def draw_shear_in(key, part):
    return shear_draw(key, 11)


def draw_shear_out(key, part):
    return shear_draw(key, 29)


def steps_of(own_key, dims, pieces, least, top_value):
    factor_of = 1.0
    for position, blocks in pieces:
        heights = jax.random.uniform(jax.random.fold_in(jax.random.fold_in(own_key, 6), position), (blocks,), jnp.float32, least / len(pieces), top_value / len(pieces))
        factor_of = factor_of * jnp.repeat(jnp.exp(heights), dims[position] // blocks).reshape((-1,) + (1,) * (len(dims) - 1 - position))
    return factor_of


def bell_draw(rng, dims, spread, bound, cuts=(), kind=jnp.bfloat16):
    drawn = jax.random.normal(rng, dims, jnp.float32) * spread
    if len(cuts) > 0:
        drawn = steps_of(rng, dims, cuts, -0.22, 0.18) * drawn
    return jnp.clip(drawn, min=-bound, max=bound).astype(kind)


def setup_inputs(seed: int = 0) -> dict:
    keys = jax.random.split(jax.random.key(seed), 7)
    vertex = bell_draw(keys[0], (HX, GX, QY, M, M), 0.2, 1.2, ((1, 2), (2, 8), (3, 2)), jnp.float32)
    bare_vertex = bell_draw(keys[1], (HX, GX, QY, M, M), 0.2, 1.2, ((1, 2), (2, 8), (3, 2)), jnp.float32)
    bubble_direct = jnp.clip(jnp.exp(math.log(1.0) - 2.3025851 * jax.random.uniform(keys[2], (HX, GX, QY, M), jnp.float32) ** steps_of(keys[2], (HX, GX, QY, M), ((1, 2), (2, 8)), -0.2, 0.2)), 0.1, 1.0)
    bubble_crossed = jnp.clip(jnp.exp(math.log(1.0) - 2.3025851 * jax.random.uniform(keys[3], (HX, GX, QY, M), jnp.float32) ** steps_of(keys[3], (HX, GX, QY, M), ((1, 2), (2, 8)), -0.2, 0.2)), 0.1, 1.0)
    shear_in = draw_shear_in(jax.random.fold_in(keys[6], 71), 0)
    shear_out = draw_shear_out(jax.random.fold_in(keys[6], 71), 0)
    return dict(vertex=vertex, bare_vertex=bare_vertex, bubble_direct=bubble_direct, bubble_crossed=bubble_crossed, shear_in=shear_in, shear_out=shear_out)


mixing = 0.5


def ladder_all(field, bubble):
    count = QX * QY
    flat_field = field.reshape(count, M, M)
    flat_bubble = bubble.reshape(count, M)

    def single(pair):
        matrix, weights = pair
        return jnp.dot(matrix * weights[None, :], matrix, precision=lax.Precision.HIGHEST, preferred_element_type=jnp.float32)

    return lax.map(single, (flat_field, flat_bubble)).reshape(QX, QY, M, M)


def crossing(field, shear_table):
    source_x = (jnp.arange(QX, dtype=jnp.int32)[:, None] - shear_table[0][None, :]) % QX
    source_y = (jnp.arange(QY, dtype=jnp.int32)[:, None] - shear_table[1][None, :]) % QY
    matrix_rows = jnp.arange(M, dtype=jnp.int32)
    return field[source_x[:, None, :], source_y[None, :, :], matrix_rows[None, None, :]]


def reference(vertex, bare_vertex, bubble_direct, bubble_crossed, shear_in, shear_out):
    field = vertex.reshape(QX, QY, M, M)
    direct_term = ladder_all(field, bubble_direct)
    crossed = crossing(field, shear_in)
    crossed_term = ladder_all(crossed, bubble_crossed)
    returned = crossing(crossed_term, shear_out)
    updated = (1.0 - mixing) * field + mixing * (bare_vertex.reshape(QX, QY, M, M) + direct_term + returned)
    return updated.reshape(HX, GX, QY, M, M)
```

```python
import functools

import jax
import jax.numpy as jnp
from jax import lax
from jax.experimental import pallas as pl
from jax.experimental.pallas import tpu as pltpu
from jax.sharding import PartitionSpec as P

mixing = 0.5
LANES = 128

VMEM = pl.BlockSpec(memory_space=pltpu.VMEM)


def call(kernel, out_shape, n_in):
    return pl.pallas_call(
        kernel,
        out_shape=out_shape,
        in_specs=[VMEM] * n_in,
        out_specs=jax.tree.map(lambda _: VMEM, out_shape),
        compiler_params=pltpu.CompilerParams(vmem_limit_bytes=56 * 1024 * 1024),
    )


def split(x):
    high = x.astype(jnp.bfloat16)
    low = (x - high.astype(jnp.float32)).astype(jnp.bfloat16)
    return high, low


def dot(a, b):
    return jnp.dot(a, b, preferred_element_type=jnp.float32)


def pick(one_hot, x):
    high, low = split(x)
    return dot(one_hot, high) + dot(one_hot, low)


def to_column(rows):
    count = rows[0].shape[1]
    stacked = jnp.concatenate(rows + [jnp.zeros((LANES - len(rows), count), jnp.float32)], axis=0)
    return stacked.T


def shear_half(table_ref, half, row_count, width_x, width_y):
    first = pl.multiple_of(half * row_count, LANES)
    shift_x = table_ref[0:1, pl.ds(first, row_count)]
    shift_y = table_ref[1:2, pl.ds(first, row_count)]
    return shift_x % width_x, shift_y % width_y, shift_x // width_x


def rank_of(label_row, label_column):
    count = label_row.shape[1]
    earlier = lax.broadcasted_iota(jnp.int32, (count, count), 0) < lax.broadcasted_iota(
        jnp.int32, (count, count), 1
    )
    same = label_column == label_row
    return jnp.sum(jnp.where(earlier & same, 1.0, 0.0), axis=0, keepdims=True)


def pack_kernel(sizes, field_ref, in_ref, out_ref, packed0_ref, packed1_ref, row_ref, column_ref):
    width_x, width_y = sizes
    items, row_count, _ = field_ref.shape
    per_class = row_count // (width_x * width_y)
    kx = lax.axis_index("kx")
    ky = lax.axis_index("ky")
    af = lax.axis_index("af")
    parts = []
    for table, half in ((in_ref, af), (in_ref, 1 - af), (out_ref, af)):
        parts.append(shear_half(table, half, row_count, width_x, width_y))
    labels = [(dx * width_y + dy).astype(jnp.float32) for dx, dy, _ in parts]
    label_columns = to_column(labels)
    rows = []
    for n, (dx, dy, turn) in enumerate(parts):
        rank = rank_of(labels[n], label_columns[:, n : n + 1]).astype(jnp.int32)
        target = ((kx + dx) % width_x) * width_y + (ky + dy) % width_y
        anchor = ((kx - dx) % width_x) * width_y + (ky - dy) % width_y
        leave = (turn + (kx + dx >= width_x).astype(jnp.int32)) % items
        arrive = (turn + (kx < dx).astype(jnp.int32)) % items
        rows.append([v.astype(jnp.float32) for v in (target * per_class + rank, anchor * per_class + rank, leave, arrive)])
    own_in, other_in, own_out = rows
    columns = to_column([own_in[1], other_in[1], own_out[1], own_out[3], own_in[2]])
    column_ref[...] = columns
    row_ref[...] = jnp.concatenate([own_in[0], own_out[0]] + [jnp.zeros((6, row_count), jnp.float32)], axis=0)
    iota = lax.broadcasted_iota(jnp.int32, (row_count, row_count), 0).astype(jnp.float32)
    one_hot = (iota == own_in[0]).astype(jnp.bfloat16)
    stay = columns[:, 4:5] == 0.0
    first, second = field_ref[0], field_ref[1]
    packed0_ref[...] = pick(one_hot, jnp.where(stay, first, second))
    packed1_ref[...] = pick(one_hot, jnp.where(stay, second, first))


def product(left, own, other):
    width = left.shape[1] // 2
    lower = lax.axis_index("af") == 0
    first = jnp.where(lower, left[:, :width], left[:, width:])
    second = jnp.where(lower, left[:, width:], left[:, :width])
    left_high, left_low = split(jnp.concatenate([first, second], axis=1))
    right_high = jnp.concatenate([own[0], other[0]], axis=0)
    right_low = jnp.concatenate([own[1], other[1]], axis=0)
    return dot(left_high, right_high) + dot(left_low, right_high) + dot(left_high, right_low)


def direct_kernel(field_ref, other_ref, bare_ref, bubble_ref, total_ref):
    for item in range(field_ref.shape[0]):
        field = field_ref[item]
        direct = product(field * bubble_ref[item : item + 1, :], split(field), split(other_ref[item]))
        total_ref[item] = (1.0 - mixing) * field + mixing * (bare_ref[item] + direct)


def unpacked(one_hot, x):
    high, low = split(x)
    return dot(one_hot, high).astype(jnp.bfloat16), dot(one_hot, low).astype(jnp.bfloat16)


def crossed_kernel(item, own_ref, other_ref, bubble_ref, row_ref, column_ref, packed_ref):
    row_count = own_ref.shape[0]
    lane = lax.broadcasted_iota(jnp.int32, (row_count, row_count), 1).astype(jnp.float32)
    sublane = lax.broadcasted_iota(jnp.int32, (row_count, row_count), 0).astype(jnp.float32)
    own = unpacked((lane == column_ref[:, 0:1]).astype(jnp.bfloat16), own_ref[...])
    other = unpacked((lane == column_ref[:, 1:2]).astype(jnp.bfloat16), other_ref[...])
    pack = (sublane == row_ref[1:2, :]).astype(jnp.bfloat16)
    left = dot(pack, own[0]) + dot(pack, own[1])
    packed_ref[...] = product(left * bubble_ref[item : item + 1, :], own, other)


def final_kernel(first_ref, second_ref, total_ref, column_ref, updated_ref):
    row_count = first_ref.shape[0]
    lane = lax.broadcasted_iota(jnp.int32, (row_count, row_count), 1).astype(jnp.float32)
    unpack = (lane == column_ref[:, 2:3]).astype(jnp.bfloat16)
    stay = column_ref[:, 3:4] == 0.0
    first = pick(unpack, first_ref[...])
    second = pick(unpack, second_ref[...])
    updated_ref[0] = total_ref[0] + mixing * jnp.where(stay, first, second)
    updated_ref[1] = total_ref[1] + mixing * jnp.where(stay, second, first)


def exchange(data):
    return lax.all_to_all(data, ("kx", "ky"), split_axis=0, concat_axis=0, tiled=True)


def swap(data):
    return lax.ppermute(data, "af", [(0, 1), (1, 0)])


def body(vertex, bare_vertex, bubble_direct, bubble_crossed, shear_in, shear_out):
    items, row_count, columns = vertex.shape[0], vertex.shape[3], vertex.shape[4]
    field = vertex.reshape(items, row_count, columns)
    bare = bare_vertex.reshape(items, row_count, columns)
    direct_bubble = bubble_direct.reshape(items, columns)
    crossed_bubble = bubble_crossed.reshape(items, columns)
    sizes = (lax.axis_size("kx"), lax.axis_size("ky"))
    whole = jax.ShapeDtypeStruct((items, row_count, columns), jnp.float32)
    block = jax.ShapeDtypeStruct((row_count, columns), jnp.float32)
    packed0, packed1, row_table, column_table = call(
        functools.partial(pack_kernel, sizes),
        (
            block,
            block,
            jax.ShapeDtypeStruct((8, row_count), jnp.float32),
            jax.ShapeDtypeStruct((row_count, LANES), jnp.float32),
        ),
        3,
    )(field, shear_in, shear_out)
    arrived0 = exchange(packed0)
    arrived1 = exchange(packed1)
    other_field = swap(field)
    total = call(direct_kernel, whole, 4)(field, other_field, bare, direct_bubble)
    back = []
    for item, arrived in enumerate((arrived0, arrived1)):
        other = swap(arrived)
        packed = call(functools.partial(crossed_kernel, item), block, 5)(
            arrived, other, crossed_bubble, row_table, column_table
        )
        back.append(exchange(packed))
    updated = call(final_kernel, whole, 4)(back[0], back[1], total, column_table)
    return updated.reshape(vertex.shape)


def solution(mesh):
    placed = (
        P(None, "kx", "ky", "af", None),
        P(None, "kx", "ky", "af", None),
        P(None, "kx", "ky", None),
        P(None, "kx", "ky", None),
        P(),
        P(),
    )
    return jax.shard_map(
        body, mesh=mesh, in_specs=placed, out_specs=P(None, "kx", "ky", "af", None), check_vma=False
    )
```
